768 devices in a mesh: polar: 8 (over x, y_lo), azimuth: 96 (over z, y_hi, core).
Axes of the slice: x: 4, y: 8 (y_hi: 4, y_lo: 2; y = y_hi * 2 + y_lo), z: 12, core: 2. Of those that a mesh axis runs over, the one named last changes fastest.
Arguments:
- state: float32 [2, 64, 72, 1440], P(None, 'polar', None, 'azimuth'), may hold values from -6 to 6
- kernels: float32 [9, 3, 9, 72], replicated, may hold values from -1.25 to 1.25
- kernel_index: int32 [32], replicated, may hold values from 0 to 8
- w_mix: float32 [72, 641], replicated, may hold values from -0.75 to 0.75
- w_in: float32 [641, 1282], replicated, may hold values from -0.25 to 0.25
- b_in: float32 [1282], replicated, may hold values from -4 to 4
- w_out: float32 [1282, 641], replicated, may hold values from -0.15625 to 0.15625
Outputs:
- encoded: float32 [2, 32, 1440, 641], P(None, 'polar', 'azimuth')
The draws below stay inside these ranges and needn't reach their ends.
All inputs are finite; a program needn't handle non-finite values.
Results may differ from the reference program's by a relative error of at most 0.000065.
Values sent between devices are 32-bit elements; how exact they have to be, the bound alone decides.
No kernel may reach another device: no remote copies, remote signals or barrier semaphores. Data moves between devices by JAX's collectives and lax.ppermute only.
A program may use at most 32 MiB of HBM per device.

```python
import jax
import jax.numpy as jnp
from jax import lax

FIELDS = 72
LON = 1440
EMBED = 641
FFN = 1282
KERNELS = 9
TAPS = 9
MEMBERS = 2
SPACING = 90
LAT = 64
LAT_OUT = 32


def touch_ends(drawn, rng, smallest, top_value):
    dims = drawn.shape
    index_at = [jax.random.randint(jax.random.fold_in(rng, axis), (), 0, dims[axis]) for axis in range(len(dims))]
    drawn = drawn.at[tuple(index_at)].set(smallest)
    longest = dims.index(max(dims))
    index_at[longest] = (index_at[longest] + 1) % dims[longest]
    return drawn.at[tuple(index_at)].set(top_value)


def block_scale(stream_key, shape, cuts, least, high):
    gain = 1.0
    for axis_at, shards_of in cuts:
        draws = jax.random.uniform(jax.random.fold_in(jax.random.fold_in(stream_key, 6), axis_at), (shards_of,), jnp.float32, least / len(cuts), high / len(cuts))
        gain = gain * jnp.repeat(jnp.exp(draws), shape[axis_at] // shards_of).reshape((-1,) + (1,) * (len(shape) - 1 - axis_at))
    return gain


def noise(stream_key, dims, width, reach, split=(), dtype=jnp.bfloat16):
    loudness = block_scale(stream_key, dims, split, -0.22, 0.18) if split else 1.0
    values = jax.random.normal(stream_key, dims, jnp.float32) * width * loudness
    return jnp.minimum(jnp.maximum(values, -reach), reach).astype(dtype)


def setup_inputs(seed: int = 0) -> dict:
    key_of = jax.random.split(jax.random.key(seed), 8)
    state = noise(key_of[0], (MEMBERS, LAT, FIELDS, LON), 1.0, 6.0, ((1, 8), (3, 96)), jnp.float32)
    kernels = noise(key_of[1], (KERNELS, 3, TAPS, FIELDS), (3 * TAPS) ** -0.5, 1.25, (), jnp.float32)
    kernel_index = touch_ends(jax.random.randint(key_of[2], (LAT_OUT,), 0, KERNELS), jax.random.fold_in(key_of[2], 1), 0, KERNELS - 1).astype(jnp.int32)
    w_mix = noise(key_of[3], (FIELDS, EMBED), FIELDS ** -0.5, 0.75, (), jnp.float32)
    w_in = noise(key_of[4], (EMBED, FFN), EMBED ** -0.5, 0.25, (), jnp.float32)
    b_in = noise(key_of[5], (FFN,), 0.7, 4.0, (), jnp.float32)
    w_out = noise(key_of[6], (FFN, EMBED), FFN ** -0.5, 0.15625, (), jnp.float32)
    return {"state": state, "kernels": kernels, "kernel_index": kernel_index, "w_mix": w_mix, "w_in": w_in, "b_in": b_in, "w_out": w_out}


def reference(state, kernels, kernel_index, w_mix, w_in, b_in, w_out):
    half = TAPS // 2
    taps = kernels[kernel_index]

    def one_member(member):
        padded = jnp.concatenate([jnp.zeros((1, FIELDS, LON), jnp.float32), member], axis=0)
        corr = jnp.zeros((LAT // 2, FIELDS, LON), jnp.float32)
        for tap_lat in range(3):
            rows = padded[tap_lat:tap_lat + LAT:2]
            for tap in range(TAPS):
                shifted = jnp.roll(rows, -(tap - half) * SPACING, axis=2)
                corr = corr + taps[:, tap_lat, tap, :, None] * shifted
        flat = jnp.transpose(corr, (0, 2, 1)).reshape(-1, FIELDS)
        mixed = jnp.dot(flat, w_mix, precision=lax.Precision.HIGHEST, preferred_element_type=jnp.float32)
        pre = jnp.dot(mixed, w_in, precision=lax.Precision.HIGHEST, preferred_element_type=jnp.float32) + b_in
        hidden = jax.nn.gelu(pre, approximate=False)
        out = mixed + jnp.dot(hidden, w_out, precision=lax.Precision.HIGHEST, preferred_element_type=jnp.float32)
        return out.reshape(LAT // 2, LON, EMBED)

    return lax.map(one_member, state)
```

```python
import functools

import jax
import jax.numpy as jnp
from jax import lax
from jax.experimental import pallas as pl
from jax.experimental.pallas import tpu as pltpu
from jax.sharding import PartitionSpec as P

SPACING = 90
VMEM = pl.BlockSpec(memory_space=pltpu.VMEM)
SMEM = pl.BlockSpec(memory_space=pltpu.SMEM)
ANY = pl.BlockSpec(memory_space=pl.ANY)
BF16 = jnp.bfloat16
F32 = jnp.float32


def ring(array, by):
    peers = lax.axis_size("azimuth")
    return lax.ppermute(array, "azimuth", [(i, (i + by) % peers) for i in range(peers)])


def next_band(array):
    peers = lax.axis_size("polar")
    return lax.ppermute(array, "polar", [(i, i + 1) for i in range(peers - 1)])


def near(array):
    return pltpu.with_memory_space_constraint(array, pltpu.VMEM)


def halves(a):
    high = a.astype(BF16)
    return high, (a - high.astype(F32)).astype(BF16)


def dot(a, b):
    return jnp.dot(a, b, preferred_element_type=F32)


def dot_t(a, b):
    return lax.dot_general(a, b, (((1,), (1,)), ((), ())), preferred_element_type=F32)


def taps_kernel(index_ref, band_ref, kern_ref, near_ref, upper_ref):
    taps, lat, _ = near_ref.shape
    outs = lat // 2
    last = index_ref.shape[0] - 1
    first = band_ref[0] * outs
    upper_ref[...] = jnp.zeros(upper_ref.shape, F32)
    for o in range(outs):
        here = index_ref[first + o]
        after = index_ref[jnp.minimum(first + o + 1, last)]
        for t in range(taps):
            near_ref[t, 2 * o : 2 * o + 2, :] = kern_ref[here, t, 1:3, :]
            upper_ref[t, 2 * o + 1 : 2 * o + 2, :] = kern_ref[after, t, 0:1, :]


def partial_kernel(x_ref, left_ref, right_ref, near_ref, upper_ref, _, *rest):
    outs, (near_s, upper_s) = rest[:3], rest[3:]
    members, lons, lat, fields = x_ref.shape
    count = members * lons
    half = lat // 2
    upper_s[0:lat, :] = jnp.zeros((lat, upper_s.shape[1]), F32)
    for s in range(3):
        base = 3 * s
        for m in range(members):
            for n in range(lons):
                i = m * lons + n
                three = (left_ref[m, n], x_ref[m, n], right_ref[m, n])
                near = three[0] * near_ref[base]
                upper = three[0] * upper_ref[base]
                for u in (1, 2):
                    near = near + three[u] * near_ref[base + u]
                    upper = upper + three[u] * upper_ref[base + u]
                near_s[i * lat : (i + 1) * lat, 0:fields] = near
                upper_s[(i + 1) * lat : (i + 2) * lat, 0:fields] = upper
        rows = count * half
        even = near_s[pl.ds(0, rows, stride=2), :]
        odd = near_s[pl.ds(1, rows, stride=2), :]
        above = upper_s[pl.ds(lat - 1, rows, stride=2), :]
        place = lax.broadcasted_iota(jnp.int32, above.shape, 0)
        above = jnp.where(place % half == 0, 0.0, above)
        outs[s][0:rows, :] = (even + odd + above)[:, 0:fields]
        halo = upper_s[pl.ds(2 * lat - 1, count, stride=lat), :]
        outs[s][rows : rows + count, :] = halo[:, 0:fields]


def in_kernel(mix_ref, in_ref, mix_h, mix_l, in_h, in_l):
    mh, ml = halves(mix_ref[...])
    wh, wl = halves(in_ref[...])
    both = dot(mh, wh) + dot(ml, wh) + dot(mh, wl)
    mix_h[...], mix_l[...] = mh, ml
    in_h[...], in_l[...] = halves(both)


def out_kernel(out_ref, out_h, out_l):
    out_h[...], out_l[...] = halves(out_ref[...])


def halo_kernel(z_ref, a_ref, b_ref, _, halo_ref):
    rows = z_ref.shape[0] - halo_ref.shape[0]
    halo_ref[...] = z_ref[rows:, :] + a_ref[rows:, :] + b_ref[rows:, :]


def fetch(pairs, sems):
    copies = [pltpu.make_async_copy(src, dst, sems.at[i]) for i, (src, dst) in enumerate(pairs)]
    for copy in copies:
        copy.start()
    return copies


def mlp(corr, mix_h, mix_l, in_h, in_l, b_in, out_h, out_l, copies):
    ch, cl = halves(corr)
    pre = dot(ch, in_h[...]) + dot(cl, in_h[...]) + dot(ch, in_l[...]) + b_in[...]
    hidden = 0.5 * pre * (1.0 + lax.erf(pre * 0.7071067811865476))
    hh, hl = halves(hidden)
    mixed = dot(ch, mix_h[...]) + dot(cl, mix_h[...]) + dot(ch, mix_l[...])
    copies[0].wait()
    total = mixed + (dot_t(hh, out_h[...]) + dot_t(hl, out_h[...]))
    copies[1].wait()
    return total + dot_t(hh, out_l[...])


def main_kernel(z_ref, a_ref, b_ref, *rest):
    weights, (oh, ol, res_ref, out_h, out_l, sems) = rest[:5], rest[5:]
    copies = fetch(((oh, out_h), (ol, out_l)), sems)
    rows = res_ref.shape[0]
    corr = z_ref[0:rows, :] + a_ref[0:rows, :] + b_ref[0:rows, :]
    res_ref[...] = mlp(corr, *weights, out_h, out_l, copies)


def edge_kernel(half, z_ref, a_ref, b_ref, halo_ref, res_ref, *rest):
    weights, (oh, ol, out_ref, scratch, out_h, out_l, sems) = rest[:5], rest[5:]
    copies = fetch(((oh, out_h), (ol, out_l)), sems)
    count = halo_ref.shape[0]
    fields = halo_ref.shape[1]
    total = z_ref[...] + a_ref[...] + b_ref[...]
    scratch[:, 0:fields] = total
    corr = scratch[pl.ds(0, count, stride=half), :][:, 0:fields] + halo_ref[...]
    members, lons = out_ref.shape[:2]
    for m in range(members):
        for n in range(lons):
            i = m * lons + n
            out_ref[m, n] = res_ref[half * i : half * (i + 1), :]
    fixed = mlp(corr, *weights, out_h, out_l, copies)
    for m in range(members):
        for n in range(lons):
            i = m * lons + n
            out_ref[m, n, 0:1, :] = fixed[i : i + 1, :]


def per_device(state, kernels, kernel_index, w_mix, w_in, b_in, w_out):
    members, lat, fields, lons = state.shape
    half = lat // 2
    count = members * lons
    rows = count * half
    taps = kernels.shape[2]
    embed, ffn = w_in.shape
    step = SPACING // lons
    S, V = jax.ShapeDtypeStruct, pltpu.VMEM

    x = jnp.transpose(state, (0, 3, 1, 2))
    left = ring(x, step)
    right = ring(x, -step)

    band = lax.axis_index("polar").astype(jnp.int32).reshape(1)
    nearby, upper = pl.pallas_call(
        taps_kernel,
        out_shape=[V((taps, lat, fields), F32)] * 2,
        in_specs=[SMEM, SMEM, VMEM],
        out_specs=[VMEM] * 2,
        name="taps",
    )(kernel_index, band, jnp.transpose(kernels, (0, 2, 1, 3)))
    mix_h, mix_l, in_h, in_l = pl.pallas_call(
        in_kernel,
        out_shape=[V((fields, embed), BF16)] * 2 + [V((fields, ffn), BF16)] * 2,
        in_specs=[VMEM] * 2,
        out_specs=[VMEM] * 4,
        name="w_in",
    )(w_mix, w_in)
    out_h, out_l = pl.pallas_call(
        out_kernel,
        out_shape=[S((embed, ffn), BF16)] * 2,
        in_specs=[VMEM],
        out_specs=[VMEM] * 2,
        name="w_out",
    )(jnp.transpose(w_out))
    bias = b_in.reshape(1, ffn)

    low, mid, high = pl.pallas_call(
        partial_kernel,
        out_shape=[V((rows + count, fields), F32)] * 3,
        in_specs=[VMEM] * 5 + [ANY],
        out_specs=[VMEM] * 3,
        scratch_shapes=[pltpu.VMEM((count * lat, 128), F32), pltpu.VMEM(((count + 1) * lat, 128), F32)],
        name="partial",
    )(x, near(left), near(right), near(nearby), near(upper), near(mix_l))
    from_high = near(ring(high, -3 * step))
    from_low = near(ring(low, 3 * step))
    mid = near(mid)

    packed = tuple(near(a) for a in (mix_h, mix_l, in_h, in_l, bias)) + (out_h, out_l)
    fetched = [pltpu.VMEM((embed, ffn), BF16)] * 2 + [pltpu.SemaphoreType.DMA((2,))]
    halo = pl.pallas_call(
        halo_kernel,
        out_shape=V((count, fields), F32),
        in_specs=[VMEM] * 3 + [ANY],
        out_specs=VMEM,
        name="halo",
    )(mid, from_high, from_low, out_l)
    halo = next_band(halo)
    res = pl.pallas_call(
        main_kernel,
        out_shape=V((rows, embed), F32),
        in_specs=[VMEM] * 8 + [ANY] * 2,
        out_specs=VMEM,
        scratch_shapes=fetched,
        name="main",
    )(mid, from_high, from_low, *packed)
    out = pl.pallas_call(
        functools.partial(edge_kernel, half),
        out_shape=S((members, lons, half, embed), F32),
        in_specs=[VMEM] * 10 + [ANY] * 2,
        out_specs=VMEM,
        scratch_shapes=[pltpu.VMEM((rows + count, 128), F32)] + fetched,
        name="edge",
    )(mid, from_high, from_low, near(halo), near(res), *packed)
    return jnp.transpose(out, (0, 2, 1, 3))


def solution(mesh):
    placed = (P(None, "polar", None, "azimuth"), P(), P(), P(), P(), P(), P())
    return jax.shard_map(
        per_device,
        mesh=mesh,
        in_specs=placed,
        out_specs=P(None, "polar", "azimuth", None),
        check_vma=False,
    )
```

```python
import functools

import jax
import jax.numpy as jnp
from jax import lax
from jax.experimental import pallas as pl
from jax.experimental.pallas import tpu as pltpu
from jax.sharding import PartitionSpec as P


SPACING = 90
LANES = 128
VMEM = pl.BlockSpec(memory_space=pltpu.VMEM)
SMEM = pl.BlockSpec(memory_space=pltpu.SMEM)
ANY = pl.BlockSpec(memory_space=pl.ANY)
BF16 = jnp.bfloat16
F32 = jnp.float32


def ring(array, by):
    peers = lax.axis_size("azimuth")
    return lax.ppermute(array, "azimuth", [(i, (i + by) % peers) for i in range(peers)])


def next_band(array):
    peers = lax.axis_size("polar")
    return lax.ppermute(array, "polar", [(i, i + 1) for i in range(peers - 1)])


def near(array):
    return pltpu.with_memory_space_constraint(array, pltpu.VMEM)


def halves(a):
    high = a.astype(BF16)
    return high, (a - high.astype(F32)).astype(BF16)


def dot(a, b):
    return jnp.dot(a, b, preferred_element_type=F32)


def dot_t(a, b):
    return lax.dot_general(a, b, (((1,), (1,)), ((), ())), preferred_element_type=F32)


def unpack(out, packed, residual, rows):
    members = 2
    lons, group, cut, rest = rows
    pad = out.shape[0] // members
    full = lons * group
    out[...] = jnp.zeros(out.shape, F32)
    out[0:full, 0:cut] = packed[0:full, 0:cut]
    out[pad : pad + full, 0:cut] = packed[0:full, cut : 2 * cut]
    for m in range(members):
        for n in range(lons):
            at = m * pad + n * group
            lane = n * rest
            out[at : at + group, cut : cut + rest] = packed[
                residual + m * group : residual + (m + 1) * group, lane : lane + rest
            ]


def pack_kernel(x_ref, out_ref):
    members, lons, lat, fields = x_ref.shape
    cut = LANES // 2
    rest = fields - cut
    for m in range(members):
        out_ref[lons + m] = jnp.zeros((lat, LANES), F32)
        for n in range(lons):
            tile = x_ref[m, n]
            out_ref[n, :, m * cut : (m + 1) * cut] = tile[:, 0:cut]
            out_ref[lons + m, :, n * rest : (n + 1) * rest] = tile[:, cut:fields]


def taps_kernel(index_ref, band_ref, kern_ref, near_ref, upper_ref, near_s, upper_s):
    taps, lat, fields = near_s.shape
    outs = lat // 2
    cut = LANES // 2
    rest = fields - cut
    last = index_ref.shape[0] - 1
    first = band_ref[0] * outs
    upper_s[...] = jnp.zeros(upper_s.shape, F32)
    for o in range(outs):
        here = index_ref[first + o]
        after = index_ref[jnp.minimum(first + o + 1, last)]
        for t in range(taps):
            near_s[t, 2 * o : 2 * o + 2, :] = kern_ref[here, t, 1:3, :]
            upper_s[t, 2 * o + 1 : 2 * o + 2, :] = kern_ref[after, t, 0:1, :]
    for src, dst in ((near_s, near_ref), (upper_s, upper_ref)):
        for t in range(taps):
            tile = src[t]
            dst[t, 0] = jnp.concatenate([tile[:, 0:cut]] * 2, axis=1)
            dst[t, 1] = jnp.concatenate([tile[:, cut:fields]] * (LANES // rest), axis=1)


def partial_kernel(x_ref, left_ref, right_ref, near_ref, upper_ref, _, *rest):
    outs, (near_s, upper_s) = rest[:3], rest[3:]
    tiles, lat, lanes = x_ref.shape
    half = lat // 2
    pairs = tiles - 2
    rows = tiles * half
    upper_s[0:lat, :] = jnp.zeros((lat, lanes), F32)
    for s in range(3):
        base = 3 * s
        for i in range(tiles):
            kind = int(i >= pairs)
            three = (left_ref[i], x_ref[i], right_ref[i])
            near = three[0] * near_ref[base, kind]
            upper = three[0] * upper_ref[base, kind]
            for u in (1, 2):
                near = near + three[u] * near_ref[base + u, kind]
                upper = upper + three[u] * upper_ref[base + u, kind]
            near_s[i * lat : (i + 1) * lat, :] = near
            upper_s[(i + 1) * lat : (i + 2) * lat, :] = upper
        even = near_s[pl.ds(0, rows, stride=2), :]
        odd = near_s[pl.ds(1, rows, stride=2), :]
        above = upper_s[pl.ds(lat - 1, rows, stride=2), :]
        place = lax.broadcasted_iota(jnp.int32, above.shape, 0)
        above = jnp.where(place % half == 0, 0.0, above)
        outs[s][0:rows, :] = even + odd + above
        outs[s][rows : rows + tiles, :] = upper_s[pl.ds(2 * lat - 1, tiles, stride=lat), :]


def spans(total, size):
    return [(at, min(size, total - at)) for at in range(0, total, size)]


def in_kernel(mix_ref, in_hbm, mix_h, mix_l, in_h, in_l, in_v, sems):
    parts = spans(in_v.shape[0], 128)
    copies = fetch([(in_hbm.at[pl.ds(*p), :], in_v.at[pl.ds(*p), :]) for p in parts], sems)
    mh, ml = halves(mix_ref[...])
    mix_h[...], mix_l[...] = mh, ml
    both = jnp.zeros(in_h.shape, F32)
    for copy, (at, size) in zip(copies, parts):
        copy.wait()
        wh, wl = halves(in_v[at : at + size, :])
        a, b = mh[:, at : at + size], ml[:, at : at + size]
        both = both + (dot(a, wh) + dot(b, wh) + dot(a, wl))
    in_h[...], in_l[...] = halves(both)


def out_kernel(out_hbm, out_h, low_hbm, out_v, low_v, sems, low_sems):
    parts = spans(out_v.shape[0], 112)
    copies = fetch([(out_hbm.at[pl.ds(*p), :], out_v.at[pl.ds(*p), :]) for p in parts], sems)
    stores = [
        pltpu.make_async_copy(low_v.at[pl.ds(*p), :], low_hbm.at[pl.ds(*p), :], low_sems.at[k])
        for k, p in enumerate(parts)
    ]
    for copy, store, (at, size) in zip(copies, stores, parts):
        copy.wait()
        out_h[at : at + size, :], low_v[at : at + size, :] = halves(out_v[at : at + size, :])
        store.start()
    for store in stores:
        store.wait()


def halo_kernel(z_ref, a_ref, b_ref, _, halo_ref):
    rows = z_ref.shape[0] - halo_ref.shape[0]
    halo_ref[...] = z_ref[rows:, :] + a_ref[rows:, :] + b_ref[rows:, :]


def fetch(pairs, sems):
    copies = [pltpu.make_async_copy(src, dst, sems.at[i]) for i, (src, dst) in enumerate(pairs)]
    for copy in copies:
        copy.start()
    return copies


def stacked(a):
    return jnp.concatenate(halves(a), axis=0)


def product(both, weight, contract):
    rows = both.shape[0] // 2
    total = contract(both, weight)
    return total[:rows] + total[rows:]


def mlp(corr_s, fields, weights, low_hbm, low_v, sems, both_s, res_s, prepare):
    mix_h, mix_l, in_h, in_l, b_in, out_h = weights
    copy = fetch(((low_hbm, low_v),), sems)[0]

    @pl.when(lax.axis_index("polar") >= 0)
    def _():
        prepare()
        both = stacked(corr_s[:, 0:fields])
        rows = corr_s.shape[0]
        pre = product(both, in_h[...], dot) + dot(both[:rows], in_l[...]) + b_in[...]
        hidden = 0.5 * pre * (1.0 + lax.erf(pre * 0.7071067811865476))
        both_s[...] = stacked(hidden)
        res_s[...] = product(both, mix_h[...], dot) + dot(both[:rows], mix_l[...])

    rows = corr_s.shape[0]
    both = both_s[...]
    total = res_s[...] + product(both, out_h[...], dot_t)
    copy.wait()
    return total + dot_t(both[:rows], low_v[...])


def main_kernel(fields, shape, z_ref, a_ref, b_ref, *rest):
    weights, (low_hbm, res_ref, sum_s, corr_s, both_s, low_v, sems) = rest[:6], rest[6:]
    lons, half = shape

    def prepare():
        sum_s[...] = z_ref[...] + a_ref[...] + b_ref[...]
        cut = LANES // 2
        unpack(corr_s, sum_s, lons * half, (lons, half, cut, fields - cut))

    res_ref[...] = mlp(corr_s, fields, weights, low_hbm, low_v, sems, both_s, res_ref, prepare)


def edge_kernel(fields, z_ref, a_ref, b_ref, halo_ref, res_ref, *rest):
    weights, (low_hbm, out_ref, sum_s, corr_s, both_s, fixed_s, low_v, sems) = rest[:6], rest[6:]
    members, lons, half, _ = out_ref.shape
    tiles = halo_ref.shape[0]
    pad = res_ref.shape[0] // members

    def prepare():
        sum_s[...] = z_ref[...] + a_ref[...] + b_ref[...]
        ends = sum_s[pl.ds(0, tiles, stride=half), :]
        sum_s[0:tiles, :] = ends + halo_ref[...]
        cut = LANES // 2
        unpack(corr_s, sum_s, lons, (lons, 1, cut, fields - cut))
        for m in range(members):
            for n in range(lons):
                at = m * pad + n * half
                out_ref[m, n] = res_ref[at : at + half, :]

    fixed = mlp(corr_s, fields, weights, low_hbm, low_v, sems, both_s, fixed_s, prepare)
    for m in range(members):
        for n in range(lons):
            at = m * (fixed.shape[0] // members) + n
            out_ref[m, n, 0:1, :] = fixed[at : at + 1, :]


def per_device(state, kernels, kernel_index, w_mix, w_in, b_in, w_out):
    members, lat, fields, lons = state.shape
    half = lat // 2
    tiles = lons + members
    taps = kernels.shape[2]
    embed, ffn = w_in.shape
    step = SPACING // lons
    S, V, DMA = jax.ShapeDtypeStruct, pltpu.VMEM, pltpu.SemaphoreType.DMA

    x = pl.pallas_call(
        pack_kernel,
        out_shape=V((tiles, lat, LANES), F32),
        in_specs=[VMEM],
        out_specs=VMEM,
        name="pack",
    )(jnp.transpose(state, (0, 3, 1, 2)))
    left = ring(x, step)
    right = ring(x, -step)

    band = lax.axis_index("polar").astype(jnp.int32).reshape(1)
    nearby, upper = pl.pallas_call(
        taps_kernel,
        out_shape=[V((taps, 2, lat, LANES), F32)] * 2,
        in_specs=[SMEM, SMEM, VMEM],
        out_specs=[VMEM] * 2,
        scratch_shapes=[V((taps, lat, fields), F32)] * 2,
        name="taps",
    )(kernel_index, band, jnp.transpose(kernels, (0, 2, 1, 3)))
    parts = len(spans(embed, 128))
    mix_h, mix_l, in_h, in_l = pl.pallas_call(
        in_kernel,
        out_shape=[V((fields, embed), BF16)] * 2 + [V((fields, ffn), BF16)] * 2,
        in_specs=[VMEM, ANY],
        out_specs=[VMEM] * 4,
        scratch_shapes=[V((embed, ffn), F32), DMA((parts,))],
        name="w_in",
    )(w_mix, w_in)
    parts = len(spans(embed, 112))
    out_h, out_l = pl.pallas_call(
        out_kernel,
        out_shape=[V((embed, ffn), BF16), S((embed, ffn), BF16)],
        in_specs=[ANY],
        out_specs=[VMEM, ANY],
        scratch_shapes=[V((embed, ffn), F32), V((embed, ffn), BF16), DMA((parts,)), DMA((parts,))],
        name="w_out",
    )(jnp.transpose(w_out))
    bias = b_in.reshape(1, ffn)

    rows = tiles * (half + 1)
    low, mid, high = pl.pallas_call(
        partial_kernel,
        out_shape=[V((rows, LANES), F32)] * 3,
        in_specs=[VMEM] * 5 + [ANY],
        out_specs=[VMEM] * 3,
        scratch_shapes=[V((tiles * lat, LANES), F32), V(((tiles + 1) * lat, LANES), F32)],
        name="partial",
    )(near(x), near(left), near(right), near(nearby), near(upper), near(mix_l))
    from_low = near(ring(low, 3 * step))
    from_high = near(ring(high, -3 * step))
    mid = near(mid)

    packed = tuple(near(a) for a in (mix_h, mix_l, in_h, in_l, bias, out_h)) + (out_l,)
    halo = pl.pallas_call(
        halo_kernel,
        out_shape=V((tiles, LANES), F32),
        in_specs=[VMEM] * 3 + [ANY],
        out_specs=VMEM,
        name="halo",
    )(mid, from_high, from_low, out_l)
    halo = next_band(halo)
    fetched = [V((embed, ffn), BF16), DMA((1,))]
    pad = members * (-(-lons * half // 16) * 16)
    res = pl.pallas_call(
        functools.partial(main_kernel, fields, (lons, half)),
        out_shape=V((pad, embed), F32),
        in_specs=[VMEM] * 9 + [ANY],
        out_specs=VMEM,
        scratch_shapes=[V((rows, LANES), F32), V((pad, LANES), F32), V((2 * pad, ffn), BF16)] + fetched,
        name="main",
    )(mid, from_high, from_low, *packed)
    pad = members * (-(-lons // 16) * 16)
    out = pl.pallas_call(
        functools.partial(edge_kernel, fields),
        out_shape=S((members, lons, half, embed), F32),
        in_specs=[VMEM] * 11 + [ANY],
        out_specs=VMEM,
        scratch_shapes=[V((rows, LANES), F32), V((pad, LANES), F32), V((2 * pad, ffn), BF16), V((pad, embed), F32)]
        + fetched,
        name="edge",
    )(mid, from_high, from_low, near(halo), near(res), *packed)
    return jnp.transpose(out, (0, 2, 1, 3))


def solution(mesh):
    placed = (P(None, "polar", None, "azimuth"), P(), P(), P(), P(), P(), P())
    return jax.shard_map(
        per_device,
        mesh=mesh,
        in_specs=placed,
        out_specs=P(None, "polar", "azimuth", None),
        check_vma=False,
    )
```

```python
import functools

import jax
import jax.numpy as jnp
from jax import lax
from jax.experimental import pallas as pl
from jax.experimental.pallas import tpu as pltpu
from jax.sharding import PartitionSpec as P


SPACING = 90
LANES = 128
KEPT = 1
VMEM = pl.BlockSpec(memory_space=pltpu.VMEM)
SMEM = pl.BlockSpec(memory_space=pltpu.SMEM)
ANY = pl.BlockSpec(memory_space=pl.ANY)
BF16 = jnp.bfloat16
F32 = jnp.float32


def ring(array, by):
    peers = lax.axis_size("azimuth")
    return lax.ppermute(array, "azimuth", [(i, (i + by) % peers) for i in range(peers)])


def next_band(array):
    peers = lax.axis_size("polar")
    return lax.ppermute(array, "polar", [(i, i + 1) for i in range(peers - 1)])


def near(array):
    return pltpu.with_memory_space_constraint(array, pltpu.VMEM)


def halves(a):
    high = a.astype(BF16)
    return high, (a - high.astype(F32)).astype(BF16)


def dot(a, b):
    return jnp.dot(a, b, preferred_element_type=F32)


def dot_t(a, b):
    return lax.dot_general(a, b, (((1,), (1,)), ((), ())), preferred_element_type=F32)


def unpack(out, packed, residual, rows):
    members = 2
    lons, group, cut, rest = rows
    pad = out.shape[0] // members
    full = lons * group
    out[...] = jnp.zeros(out.shape, F32)
    out[0:full, 0:cut] = packed[0:full, 0:cut]
    out[pad : pad + full, 0:cut] = packed[0:full, cut : 2 * cut]
    for m in range(members):
        for n in range(lons):
            at = m * pad + n * group
            lane = n * rest
            out[at : at + group, cut : cut + rest] = packed[
                residual + m * group : residual + (m + 1) * group, lane : lane + rest
            ]


def pack_kernel(x_ref, out_ref):
    members, lons, lat, fields = x_ref.shape
    cut = LANES // 2
    rest = fields - cut
    for m in range(members):
        out_ref[lons + m] = jnp.zeros((lat, LANES), F32)
        for n in range(lons):
            tile = x_ref[m, n]
            out_ref[n, :, m * cut : (m + 1) * cut] = tile[:, 0:cut]
            out_ref[lons + m, :, n * rest : (n + 1) * rest] = tile[:, cut:fields]


def taps_kernel(index_ref, band_ref, kern_ref, near_ref, upper_ref, near_s, upper_s):
    taps, lat, fields = near_s.shape
    outs = lat // 2
    cut = LANES // 2
    rest = fields - cut
    last = index_ref.shape[0] - 1
    first = band_ref[0] * outs
    upper_s[...] = jnp.zeros(upper_s.shape, F32)
    for o in range(outs):
        here = index_ref[first + o]
        after = index_ref[jnp.minimum(first + o + 1, last)]
        for t in range(taps):
            near_s[t, 2 * o : 2 * o + 2, :] = kern_ref[here, t, 1:3, :]
            upper_s[t, 2 * o + 1 : 2 * o + 2, :] = kern_ref[after, t, 0:1, :]
    for src, dst in ((near_s, near_ref), (upper_s, upper_ref)):
        for t in range(taps):
            tile = src[t]
            dst[t, 0] = jnp.concatenate([tile[:, 0:cut]] * 2, axis=1)
            dst[t, 1] = jnp.concatenate([tile[:, cut:fields]] * (LANES // rest), axis=1)


def partial_kernel(x_ref, left_ref, right_ref, near_ref, upper_ref, _, *rest):
    outs, (halo_ref, near_s, upper_s) = rest[:3], rest[3:]
    tiles, lat, lanes = x_ref.shape
    half = lat // 2
    pairs = tiles - 2
    rows = tiles * half
    upper_s[0:lat, :] = jnp.zeros((lat, lanes), F32)
    for s in range(3):
        base = 3 * s
        for i in range(tiles):
            kind = int(i >= pairs)
            three = (left_ref[i], x_ref[i], right_ref[i])
            near = three[0] * near_ref[base, kind]
            upper = three[0] * upper_ref[base, kind]
            for u in (1, 2):
                near = near + three[u] * near_ref[base + u, kind]
                upper = upper + three[u] * upper_ref[base + u, kind]
            near_s[i * lat : (i + 1) * lat, :] = near
            upper_s[(i + 1) * lat : (i + 2) * lat, :] = upper
        even = near_s[pl.ds(0, rows, stride=2), :]
        odd = near_s[pl.ds(1, rows, stride=2), :]
        above = upper_s[pl.ds(lat - 1, rows, stride=2), :]
        place = lax.broadcasted_iota(jnp.int32, above.shape, 0)
        above = jnp.where(place % half == 0, 0.0, above)
        outs[s][...] = even + odd + above
        halo_ref[s * tiles : (s + 1) * tiles, :] = upper_s[pl.ds(2 * lat - 1, tiles, stride=lat), :]


def spans(total, size):
    return [(at, min(size, total - at)) for at in range(0, total, size)]


def in_kernel(mix_ref, in_hbm, mix_h, mix_l, in_h, in_l, in_v, both_s, sems):
    parts = spans(in_v.shape[0], 256)
    copies = fetch([(in_hbm.at[pl.ds(*p), :], in_v.at[pl.ds(*p), :]) for p in parts], sems)
    rows = mix_ref.shape[0]
    pad = both_s.shape[0] // 2
    mh, ml = halves(mix_ref[...])
    mix_h[...], mix_l[...] = mh, ml
    both_s[...] = jnp.zeros(both_s.shape, BF16)
    both_s[0:rows, :] = mh
    both_s[pad : pad + rows, :] = ml
    total = jnp.zeros(in_h.shape, F32)
    for copy, (at, size) in zip(copies, parts):
        copy.wait()
        wh, wl = halves(in_v[at : at + size, :])
        two = dot(both_s[:, at : at + size], wh)
        total = total + (two[0:rows] + two[pad : pad + rows] + dot(both_s[0:rows, at : at + size], wl))
    in_h[...], in_l[...] = halves(total)


def out_kernel(out_hbm, _, *rest):
    pieces, (low_hbm, down_ref, side_ref, out_v, low_v, sems, low_sems) = rest[:-7], rest[-7:]
    depth = low_v.shape[1]
    blocks = out_v.shape[0] // LANES
    parts = list(reversed(spans(out_v.shape[0], LANES)))
    copies = fetch([(out_hbm.at[pl.ds(*p), :], out_v.at[pl.ds(*p), :]) for p in parts], sems)
    stores = []
    for copy, (at, size) in zip(copies, parts):
        copy.wait()
        block = at // LANES
        if block == blocks:
            continue
        high, low = halves(out_v[at : at + size, 0:depth])
        pieces[block][...] = high
        if block < KEPT:
            pieces[blocks + block][...] = low
            continue
        view = pl.ds(at - KEPT * LANES, size)
        low_v[view, :] = low
        store = pltpu.make_async_copy(low_v.at[view, :], low_hbm.at[view, :], low_sems.at[len(stores)])
        store.start()
        stores.append(store)
    down_ref[...] = jnp.transpose(out_v[:, depth:])
    side_ref[...] = out_v[blocks * LANES :, :]
    for store in stores:
        store.wait()


def join_kernel(low_ref, mid_ref, high_ref, halo_ref, _, *outs):
    tiles = halo_ref.shape[0] // 3
    half = low_ref.shape[0] // tiles
    for s, (src, dst) in enumerate(zip((low_ref, mid_ref, high_ref), outs)):
        dst[...] = src[...]
        view = pl.ds(0, tiles, stride=half)
        dst[view, :] = src[view, :] + halo_ref[s * tiles : (s + 1) * tiles, :]


def fetch(pairs, sems):
    copies = [pltpu.make_async_copy(src, dst, sems.at[i]) for i, (src, dst) in enumerate(pairs)]
    for copy in copies:
        copy.start()
    return copies


def stacked(a):
    return jnp.concatenate(halves(a), axis=0)


def product(both, weight, contract):
    rows = both.shape[0] // 2
    total = contract(both, weight)
    return total[:rows] + total[rows:]


def main_kernel(shape, z_ref, a_ref, b_ref, *rest):
    mix_h, mix_l, in_h, in_l, b_in, down, side = rest[:7]
    pieces, rest = rest[7:-10], rest[-10:]
    low_hbm, out_hbm, sum_s, corr_s, both_s, res_s, low_v, out_v, sems, out_sems = rest
    members, lons, half, embed = out_v.shape
    fields = shape
    blocks = embed // LANES
    count, depth = blocks * LANES, low_v.shape[1]
    kept = KEPT * LANES
    parts = [(0, kept)] + [(kept + at, size) for at, size in spans(count - kept, 256)]
    views = [pl.ds(at - kept, size) for at, size in parts[1:]]
    lows = fetch([(low_hbm.at[v, :], low_v.at[v, :]) for v in views], sems)
    rows = corr_s.shape[0]

    @pl.when(lax.axis_index("polar") >= 0)
    def _():
        sum_s[...] = z_ref[...] + a_ref[...] + b_ref[...]
        cut = LANES // 2
        unpack(corr_s, sum_s, lons * half, (lons, half, cut, fields - cut))
        both = stacked(corr_s[:, 0:fields])
        pre = product(both, in_h[...], dot) + dot(both[:rows], in_l[...]) + b_in[...]
        hidden = 0.5 * pre * (1.0 + lax.erf(pre * 0.7071067811865476))
        both_s[...] = stacked(hidden[:, 0:depth])
        mixed = product(both, mix_h[...], dot) + dot(both[:rows], mix_l[...])
        for k in range(down.shape[0]):
            mixed = mixed + hidden[:, depth + k : depth + k + 1] * down[k : k + 1, :]
        res_s[...] = mixed
        last = jnp.sum(hidden[:, 0:depth] * side[:, 0:depth], axis=1, keepdims=True)
        res_s[:, count : count + 1] = mixed[:, count : count + 1] + last

    stores = []
    for k, (at, size) in enumerate(parts):
        first = at // LANES
        held = [pieces[b][...] for b in range(first, first + size // LANES)]
        total = product(both_s[...], jnp.concatenate(held, axis=0), dot_t)
        if at < kept:
            held = [pieces[blocks + b][...] for b in range(first, first + size // LANES)]
            low = jnp.concatenate(held, axis=0)
        else:
            lows[k - 1].wait()
            low = low_v[at - kept : at - kept + size, :]
        res_s[:, at : at + size] += total + dot_t(both_s[0:rows, :], low)
        end = embed if k == len(parts) - 1 else at + size
        for m in range(members):
            for n in range(lons):
                row = m * (rows // members) + n * half
                out_v[m, n, :, at:end] = res_s[row : row + half, at:end]
        lanes = pl.ds(at, end - at)
        store = pltpu.make_async_copy(out_v.at[:, :, :, lanes], out_hbm.at[:, :, :, lanes], out_sems.at[k])
        store.start()
        stores.append(store)
    for store in stores:
        store.wait()


def per_device(state, kernels, kernel_index, w_mix, w_in, b_in, w_out):
    members, lat, fields, lons = state.shape
    half = lat // 2
    tiles = lons + members
    taps = kernels.shape[2]
    embed, ffn = w_in.shape
    step = SPACING // lons
    S, V, DMA = jax.ShapeDtypeStruct, pltpu.VMEM, pltpu.SemaphoreType.DMA

    x = pl.pallas_call(
        pack_kernel,
        out_shape=V((tiles, lat, LANES), F32),
        in_specs=[VMEM],
        out_specs=VMEM,
        name="pack",
    )(jnp.transpose(state, (0, 3, 1, 2)))
    left = ring(x, step)
    right = ring(x, -step)

    band = lax.axis_index("polar").astype(jnp.int32).reshape(1)
    nearby, upper = pl.pallas_call(
        taps_kernel,
        out_shape=[V((taps, 2, lat, LANES), F32)] * 2,
        in_specs=[SMEM, SMEM, VMEM],
        out_specs=[VMEM] * 2,
        scratch_shapes=[V((taps, lat, fields), F32)] * 2,
        name="taps",
    )(kernel_index, band, jnp.transpose(kernels, (0, 2, 1, 3)))
    parts = len(spans(embed, 256))
    mix_h, mix_l, in_h, in_l = pl.pallas_call(
        in_kernel,
        out_shape=[V((fields, embed), BF16)] * 2 + [V((fields, ffn), BF16)] * 2,
        in_specs=[VMEM, ANY],
        out_specs=[VMEM] * 4,
        scratch_shapes=[V((embed, ffn), F32), V((2 * (-(-fields // 16) * 16), embed), BF16), DMA((parts,))],
        name="w_in",
    )(w_mix, w_in)
    bias = b_in.reshape(1, ffn)

    rows = tiles * half
    low, mid, high, halo = pl.pallas_call(
        partial_kernel,
        out_shape=[V((rows, LANES), F32)] * 3 + [V((3 * tiles, LANES), F32)],
        in_specs=[VMEM] * 5 + [ANY],
        out_specs=[VMEM] * 4,
        scratch_shapes=[V((tiles * lat, LANES), F32), V(((tiles + 1) * lat, LANES), F32)],
        name="partial",
    )(near(x), near(left), near(right), near(nearby), near(upper), near(mix_l))
    above = next_band(halo)

    blocks, depth = embed // LANES, ffn // LANES * LANES
    count = blocks * LANES
    fetched = (blocks - KEPT) * LANES
    parts = len(spans(embed, LANES))
    *pieces, low_w, down, side = pl.pallas_call(
        out_kernel,
        out_shape=[V((LANES, depth), BF16)] * (blocks + KEPT)
        + [S((fetched, depth), BF16), V((ffn - depth, embed), F32), V((embed - count, ffn), F32)],
        in_specs=[ANY] * 2,
        out_specs=[VMEM] * (blocks + KEPT) + [ANY, VMEM, VMEM],
        scratch_shapes=[V((embed, ffn), F32), V((fetched, depth), BF16), DMA((parts,)), DMA((parts,))],
        name="w_out",
    )(jnp.transpose(w_out), near(halo))
    low, mid, high = pl.pallas_call(
        join_kernel,
        out_shape=[V((rows, LANES), F32)] * 3,
        in_specs=[VMEM] * 4 + [ANY],
        out_specs=[VMEM] * 3,
        name="join",
    )(near(low), near(mid), near(high), near(above), near(side))
    from_low = ring(low, 3 * step)
    from_high = ring(high, -3 * step)

    pad = members * (-(-lons * half // 16) * 16)
    out = pl.pallas_call(
        functools.partial(main_kernel, fields),
        out_shape=S((members, lons, half, embed), F32),
        in_specs=[VMEM] * (10 + blocks + KEPT) + [ANY],
        out_specs=ANY,
        scratch_shapes=[
            V((rows, LANES), F32),
            V((pad, LANES), F32),
            V((2 * pad, depth), BF16),
            V((pad, embed), F32),
            V((fetched, depth), BF16),
            V((members, lons, half, embed), F32),
            DMA((1 + len(spans(fetched, 256)),)),
            DMA((1 + len(spans(fetched, 256)),)),
        ],
        name="main",
    )(*(near(a) for a in (mid, from_low, from_high, mix_h, mix_l, in_h, in_l, bias, down, side, *pieces)), low_w)
    return jnp.transpose(out, (0, 2, 1, 3))


def solution(mesh):
    placed = (P(None, "polar", None, "azimuth"), P(), P(), P(), P(), P(), P())
    return jax.shard_map(
        per_device,
        mesh=mesh,
        in_specs=placed,
        out_specs=P(None, "polar", "azimuth", None),
        check_vma=False,
    )
```

```python
import functools

import jax
import jax.numpy as jnp
from jax import lax
from jax.experimental import pallas as pl
from jax.experimental.pallas import tpu as pltpu
from jax.sharding import PartitionSpec as P


SPACING = 90
LANES = 128
VMEM = pl.BlockSpec(memory_space=pltpu.VMEM)
SMEM = pl.BlockSpec(memory_space=pltpu.SMEM)
ANY = pl.BlockSpec(memory_space=pl.ANY)
BF16 = jnp.bfloat16
F32 = jnp.float32


call = functools.partial(pl.pallas_call, compiler_params=pltpu.CompilerParams(vmem_limit_bytes=24 << 20))


def ring(array, by):
    peers = lax.axis_size("azimuth")
    return lax.ppermute(array, "azimuth", [(i, (i + by) % peers) for i in range(peers)])


def next_band(array):
    peers = lax.axis_size("polar")
    return lax.ppermute(array, "polar", [(i, i + 1) for i in range(peers - 1)])


def near(array):
    return pltpu.with_memory_space_constraint(array, pltpu.VMEM)


def far(array):
    return pltpu.with_memory_space_constraint(array, pltpu.HBM)


def halves(a):
    high = a.astype(BF16)
    return high, (a - high.astype(F32)).astype(BF16)


def dot(a, b):
    return jnp.dot(a, b, preferred_element_type=F32)


def dot_t(a, b):
    return lax.dot_general(a, b, (((1,), (1,)), ((), ())), preferred_element_type=F32)


def unpack(out, packed, residual, rows):
    members = 2
    lons, group, cut, rest = rows
    pad = out.shape[0] // members
    full = lons * group
    out[...] = jnp.zeros(out.shape, F32)
    out[0:full, 0:cut] = packed[0:full, 0:cut]
    out[pad : pad + full, 0:cut] = packed[0:full, cut : 2 * cut]
    for m in range(members):
        for n in range(lons):
            at = m * pad + n * group
            lane = n * rest
            out[at : at + group, cut : cut + rest] = packed[
                residual + m * group : residual + (m + 1) * group, lane : lane + rest
            ]


def pack_kernel(x_ref, out_ref):
    members, lons, lat, fields = x_ref.shape
    cut = LANES // 2
    rest = fields - cut
    for m in range(members):
        out_ref[lons + m] = jnp.zeros((lat, LANES), F32)
        for n in range(lons):
            tile = x_ref[m, n]
            out_ref[n, :, m * cut : (m + 1) * cut] = tile[:, 0:cut]
            out_ref[lons + m, :, n * rest : (n + 1) * rest] = tile[:, cut:fields]


def taps_kernel(index_ref, kern_ref, near_ref, upper_ref, near_s, upper_s):
    taps, lat, fields = near_s.shape
    outs = lat // 2
    cut = LANES // 2
    rest = fields - cut
    last = index_ref.shape[0] - 1
    first = lax.axis_index("polar") * outs
    upper_s[...] = jnp.zeros(upper_s.shape, F32)
    for o in range(outs):
        here = index_ref[first + o]
        after = index_ref[jnp.minimum(first + o + 1, last)]
        for t in range(taps):
            near_s[t, 2 * o : 2 * o + 2, :] = kern_ref[here, t, 1:3, :]
            upper_s[t, 2 * o + 1 : 2 * o + 2, :] = kern_ref[after, t, 0:1, :]
    for src, dst in ((near_s, near_ref), (upper_s, upper_ref)):
        for t in range(taps):
            tile = src[t]
            dst[t, 0] = jnp.concatenate([tile[:, 0:cut]] * 2, axis=1)
            dst[t, 1] = jnp.concatenate([tile[:, cut:fields]] * (LANES // rest), axis=1)


def partial_kernel(x_ref, left_ref, right_ref, near_ref, upper_ref, _, *rest):
    outs, (halo_ref, near_s, upper_s) = rest[:3], rest[3:]
    tiles, lat, lanes = x_ref.shape
    half = lat // 2
    pairs = tiles - 2
    rows = tiles * half
    upper_s[0:lat, :] = jnp.zeros((lat, lanes), F32)
    for s in range(3):
        base = 3 * s
        for i in range(tiles):
            kind = int(i >= pairs)
            three = (left_ref[i], x_ref[i], right_ref[i])
            near = three[0] * near_ref[base, kind]
            upper = three[0] * upper_ref[base, kind]
            for u in (1, 2):
                near = near + three[u] * near_ref[base + u, kind]
                upper = upper + three[u] * upper_ref[base + u, kind]
            near_s[i * lat : (i + 1) * lat, :] = near
            upper_s[(i + 1) * lat : (i + 2) * lat, :] = upper
        even = near_s[pl.ds(0, rows, stride=2), :]
        odd = near_s[pl.ds(1, rows, stride=2), :]
        above = upper_s[pl.ds(lat - 1, rows, stride=2), :]
        place = lax.broadcasted_iota(jnp.int32, above.shape, 0)
        above = jnp.where(place % half == 0, 0.0, above)
        outs[s][...] = even + odd + above
        halo_ref[s * tiles : (s + 1) * tiles, :] = upper_s[pl.ds(2 * lat - 1, tiles, stride=lat), :]


def in_kernel(mix_ref, in_hbm, mix_s, in_s, both_s, in_v, sems):
    parts = [(at, min(256, in_v.shape[0] - at)) for at in range(0, in_v.shape[0], 256)]
    copies = []
    for k, part in enumerate(parts):
        view = pl.ds(*part)
        copies.append(pltpu.make_async_copy(in_hbm.at[view, :], in_v.at[view, :], sems.at[k]))
        copies[-1].start()
    rows = mix_ref.shape[0]
    pad = both_s.shape[0] // 2
    mh, ml = halves(mix_ref[...])
    for k, part in enumerate((mh, mh, ml)):
        mix_s[k * pad : (k + 1) * pad, :] = jnp.zeros((pad, mix_s.shape[1]), BF16)
        mix_s[k * pad : k * pad + rows, :] = part
    both_s[...] = jnp.zeros(both_s.shape, BF16)
    both_s[0:rows, :] = mh
    both_s[pad : pad + rows, :] = ml
    total = jnp.zeros((pad, in_v.shape[1]), F32)
    for copy, (at, size) in zip(copies, parts):
        copy.wait()
        wh, wl = halves(in_v[at : at + size, :])
        both = both_s[:, at : at + size]
        two = dot(both, wh)
        total = total + (two[0:pad] + two[pad : 2 * pad] + dot(both[0:pad], wl))
    high, low = halves(total)
    for k, part in enumerate((high, high, low)):
        in_s[k * pad : (k + 1) * pad, :] = part


def out_kernel(out_ref, _, out_h, out_l, down_ref, side_ref):
    count, depth = out_h.shape
    out_h[...], out_l[...] = halves(out_ref[0:count, 0:depth])
    down_ref[...] = jnp.transpose(out_ref[:, depth:])
    side_ref[...] = out_ref[count:, :]


def join_kernel(low_ref, mid_ref, high_ref, halo_ref, _, *outs):
    tiles = halo_ref.shape[0] // 3
    half = low_ref.shape[0] // tiles
    for s, (src, dst) in enumerate(zip((low_ref, mid_ref, high_ref), outs)):
        view = pl.ds(0, tiles, stride=half)
        dst[view, :] = src[view, :] + halo_ref[s * tiles : (s + 1) * tiles, :]


def stacked(a):
    return jnp.concatenate(halves(a), axis=0)


def product(both, weight, contract):
    rows = both.shape[0] // 2
    total = contract(both, weight)
    return total[:rows] + total[rows:]


def main_kernel(fields, z_ref, a_ref, b_ref, mix_ref, in_ref, b_in, down, side, out_h, out_l, out_ref, sum_s, corr_s, both_s):
    members, lons, half, _ = out_ref.shape
    count, depth = out_h.shape
    rows = corr_s.shape[0]
    pad = in_ref.shape[0] // 3
    sum_s[...] = z_ref[...] + a_ref[...] + b_ref[...]
    cut = LANES // 2
    unpack(corr_s, sum_s, lons * half, (lons, half, cut, fields - cut))
    high, low = halves(corr_s[:, 0:fields])
    both_s[...] = jnp.zeros(both_s.shape, BF16)
    for k, part in enumerate((high, low, high)):
        both_s[:, k * pad : k * pad + fields] = part
    corr = both_s[:, 0 : 3 * pad]
    pre = dot(corr, in_ref[...]) + b_in[...]
    hidden = 0.5 * pre * (1.0 + lax.erf(pre * 0.7071067811865476))
    both = stacked(hidden[:, 0:depth])
    res = dot(corr, mix_ref[...])
    for k in range(down.shape[0]):
        res = res + hidden[:, depth + k : depth + k + 1] * down[k : k + 1, :]
    last = jnp.sum(hidden[:, 0:depth] * side[:, 0:depth], axis=1, keepdims=True)
    last = res[:, count : count + 1] + last
    res = res[:, 0:count] + product(both, out_h[...], dot_t) + dot_t(both[:rows], out_l[...])
    for m in range(members):
        for n in range(lons):
            row = m * (rows // members) + n * half
            out_ref[m, n, :, 0:count] = res[row : row + half]
            out_ref[m, n, :, count : count + 1] = last[row : row + half]


def per_device(state, kernels, kernel_index, w_mix, w_in, b_in, w_out):
    members, lat, fields, lons = state.shape
    half = lat // 2
    tiles = lons + members
    taps = kernels.shape[2]
    embed, ffn = w_in.shape
    step = SPACING // lons
    S, V = jax.ShapeDtypeStruct, pltpu.VMEM

    x = call(
        pack_kernel,
        out_shape=V((tiles, lat, LANES), F32),
        in_specs=[VMEM],
        out_specs=VMEM,
        name="pack",
    )(far(jnp.transpose(state, (0, 3, 1, 2))))
    left = ring(x, step)
    right = ring(x, -step)

    nearby, upper = call(
        taps_kernel,
        out_shape=[V((taps, 2, lat, LANES), F32)] * 2,
        in_specs=[SMEM, VMEM],
        out_specs=[VMEM] * 2,
        scratch_shapes=[V((taps, lat, fields), F32)] * 2,
        name="taps",
    )(far(kernel_index), far(jnp.transpose(kernels, (0, 2, 1, 3))))
    deep = -(-fields // 16) * 16
    mix_s, in_s = call(
        in_kernel,
        out_shape=[V((3 * deep, embed), BF16), V((3 * deep, ffn), BF16)],
        in_specs=[VMEM, ANY],
        out_specs=[VMEM] * 2,
        scratch_shapes=[V((2 * deep, embed), BF16), V((embed, ffn), F32), pltpu.SemaphoreType.DMA((-(-embed // 256),))],
        name="w_in",
    )(far(w_mix), far(w_in))
    bias = b_in.reshape(1, ffn)

    rows = tiles * half
    low, mid, high, halo = call(
        partial_kernel,
        out_shape=[V((rows, LANES), F32)] * 3 + [V((3 * tiles, LANES), F32)],
        in_specs=[VMEM] * 5 + [ANY],
        out_specs=[VMEM] * 4,
        scratch_shapes=[V((tiles * lat, LANES), F32), V(((tiles + 1) * lat, LANES), F32)],
        name="partial",
    )(near(x), near(left), near(right), near(nearby), near(upper), near(mix_s))
    above = next_band(halo)

    count, depth = embed // LANES * LANES, ffn // LANES * LANES
    out_h, out_l, down, side = call(
        out_kernel,
        out_shape=[V((count, depth), BF16)] * 2 + [V((ffn - depth, embed), F32), V((embed - count, ffn), F32)],
        in_specs=[VMEM, ANY],
        out_specs=[VMEM] * 4,
        name="w_out",
    )(near(jnp.transpose(w_out)), near(halo))
    low, mid, high = call(
        join_kernel,
        out_shape=[V((rows, LANES), F32)] * 3,
        in_specs=[VMEM] * 4 + [ANY],
        out_specs=[VMEM] * 3,
        input_output_aliases={0: 0, 1: 1, 2: 2},
        name="join",
    )(near(low), near(mid), near(high), near(above), near(side))
    from_low = ring(low, 3 * step)
    from_high = ring(high, -3 * step)

    pad = members * (-(-lons * half // 16) * 16)
    out = call(
        functools.partial(main_kernel, fields),
        out_shape=S((members, lons, half, embed), F32),
        in_specs=[VMEM] * 10,
        out_specs=VMEM,
        scratch_shapes=[V((rows, LANES), F32), V((pad, LANES), F32), V((pad, 2 * LANES), BF16)],
        name="main",
    )(*(near(a) for a in (mid, from_low, from_high, mix_s, in_s, bias, down, side, out_h, out_l)))
    return jnp.transpose(out, (0, 2, 1, 3))


def solution(mesh):
    placed = (P(None, "polar", None, "azimuth"), P(), P(), P(), P(), P(), P())
    return jax.shard_map(
        per_device,
        mesh=mesh,
        in_specs=placed,
        out_specs=P(None, "polar", "azimuth", None),
        check_vma=False,
    )
```

```python
import functools

import jax
import jax.numpy as jnp
from jax import lax
from jax.experimental import pallas as pl
from jax.experimental.pallas import tpu as pltpu
from jax.sharding import PartitionSpec as P


SPACING = 90
LANES = 128
VMEM = pl.BlockSpec(memory_space=pltpu.VMEM)
SMEM = pl.BlockSpec(memory_space=pltpu.SMEM)
ANY = pl.BlockSpec(memory_space=pl.ANY)
BF16 = jnp.bfloat16
F32 = jnp.float32


call = functools.partial(pl.pallas_call, compiler_params=pltpu.CompilerParams(vmem_limit_bytes=24 << 20))


def ring(array, by):
    peers = lax.axis_size("azimuth")
    return lax.ppermute(array, "azimuth", [(i, (i + by) % peers) for i in range(peers)])


def next_band(array):
    peers = lax.axis_size("polar")
    return lax.ppermute(array, "polar", [(i, i + 1) for i in range(peers - 1)])


def near(array):
    return pltpu.with_memory_space_constraint(array, pltpu.VMEM)


def far(array):
    return pltpu.with_memory_space_constraint(array, pltpu.HBM)


def halves(a):
    high = a.astype(BF16)
    return high, (a - high.astype(F32)).astype(BF16)


def dot(a, b):
    return jnp.dot(a, b, preferred_element_type=F32)


def unpack(out, packed, residual, rows):
    members = 2
    lons, group, cut, rest = rows
    pad = out.shape[0] // members
    full = lons * group
    out[...] = jnp.zeros(out.shape, F32)
    out[0:full, 0:cut] = packed[0:full, 0:cut]
    out[pad : pad + full, 0:cut] = packed[0:full, cut : 2 * cut]
    for m in range(members):
        for n in range(lons):
            at = m * pad + n * group
            lane = n * rest
            out[at : at + group, cut : cut + rest] = packed[
                residual + m * group : residual + (m + 1) * group, lane : lane + rest
            ]


def pack_kernel(x_ref, out_ref):
    members, lons, lat, fields = x_ref.shape
    cut = LANES // 2
    rest = fields - cut
    for m in range(members):
        out_ref[lons + m] = jnp.zeros((lat, LANES), F32)
        for n in range(lons):
            tile = x_ref[m, n]
            out_ref[n, :, m * cut : (m + 1) * cut] = tile[:, 0:cut]
            out_ref[lons + m, :, n * rest : (n + 1) * rest] = tile[:, cut:fields]


def taps_kernel(index_ref, kern_ref, near_ref, upper_ref, near_s, upper_s):
    taps, lat, fields = near_s.shape
    outs = lat // 2
    cut = LANES // 2
    rest = fields - cut
    last = index_ref.shape[0] - 1
    first = lax.axis_index("polar") * outs
    upper_s[...] = jnp.zeros(upper_s.shape, F32)
    for o in range(outs):
        here = index_ref[first + o]
        after = index_ref[jnp.minimum(first + o + 1, last)]
        for t in range(taps):
            near_s[t, 2 * o : 2 * o + 2, :] = kern_ref[here, t, 1:3, :]
            upper_s[t, 2 * o + 1 : 2 * o + 2, :] = kern_ref[after, t, 0:1, :]
    for src, dst in ((near_s, near_ref), (upper_s, upper_ref)):
        for t in range(taps):
            tile = src[t]
            dst[t, 0] = jnp.concatenate([tile[:, 0:cut]] * 2, axis=1)
            dst[t, 1] = jnp.concatenate([tile[:, cut:fields]] * (LANES // rest), axis=1)


def partial_kernel(x_ref, left_ref, right_ref, near_ref, upper_ref, _, *rest):
    outs, (halo_ref, near_s, upper_s) = rest[:3], rest[3:]
    tiles, lat, lanes = x_ref.shape
    half = lat // 2
    pairs = tiles - 2
    rows = tiles * half
    upper_s[0:lat, :] = jnp.zeros((lat, lanes), F32)
    for s in range(3):
        base = 3 * s
        for i in range(tiles):
            kind = int(i >= pairs)
            three = (left_ref[i], x_ref[i], right_ref[i])
            near = three[0] * near_ref[base, kind]
            upper = three[0] * upper_ref[base, kind]
            for u in (1, 2):
                near = near + three[u] * near_ref[base + u, kind]
                upper = upper + three[u] * upper_ref[base + u, kind]
            near_s[i * lat : (i + 1) * lat, :] = near
            upper_s[(i + 1) * lat : (i + 2) * lat, :] = upper
        even = near_s[pl.ds(0, rows, stride=2), :]
        odd = near_s[pl.ds(1, rows, stride=2), :]
        above = upper_s[pl.ds(lat - 1, rows, stride=2), :]
        place = lax.broadcasted_iota(jnp.int32, above.shape, 0)
        above = jnp.where(place % half == 0, 0.0, above)
        outs[s][...] = even + odd + above
        halo_ref[s * tiles : (s + 1) * tiles, :] = upper_s[pl.ds(2 * lat - 1, tiles, stride=lat), :]


def in_kernel(mix_ref, in_hbm, mix_s, in_s, both_s, in_v, sems):
    parts = [(at, min(256, in_v.shape[0] - at)) for at in range(0, in_v.shape[0], 256)]
    copies = []
    for k, part in enumerate(parts):
        view = pl.ds(*part)
        copies.append(pltpu.make_async_copy(in_hbm.at[view, :], in_v.at[view, :], sems.at[k]))
        copies[-1].start()
    rows = mix_ref.shape[0]
    pad = both_s.shape[0] // 2
    mh, ml = halves(mix_ref[...])
    for k, part in enumerate((mh, mh, ml)):
        mix_s[k * pad : (k + 1) * pad, :] = jnp.zeros((pad, mix_s.shape[1]), BF16)
        mix_s[k * pad : k * pad + rows, :] = part
    both_s[...] = jnp.zeros(both_s.shape, BF16)
    both_s[0:rows, :] = mh
    both_s[pad : pad + rows, :] = ml
    total = jnp.zeros((pad, in_v.shape[1]), F32)
    for copy, (at, size) in zip(copies, parts):
        copy.wait()
        wh, wl = halves(in_v[at : at + size, :])
        both = both_s[:, at : at + size]
        two = dot(both, wh)
        total = total + (two[0:pad] + two[pad : 2 * pad] + dot(both[0:pad], wl))
    high, low = halves(total)
    for k, part in enumerate((high, high, low)):
        in_s[k * pad : (k + 1) * pad, :] = part


def out_kernel(out_ref, _, out_h, out_l, down_ref, side_ref):
    depth, count = out_h.shape
    out_h[...], out_l[...] = halves(jnp.transpose(out_ref[0:count, 0:depth]))
    down_ref[...] = jnp.transpose(out_ref[:, depth:])
    side_ref[...] = out_ref[count:, :]


def join_kernel(low_ref, mid_ref, high_ref, halo_ref, _, *outs):
    tiles = halo_ref.shape[0] // 3
    half = low_ref.shape[0] // tiles
    for s, (src, dst) in enumerate(zip((low_ref, mid_ref, high_ref), outs)):
        view = pl.ds(0, tiles, stride=half)
        dst[view, :] = src[view, :] + halo_ref[s * tiles : (s + 1) * tiles, :]


def stacked(a):
    return jnp.concatenate(halves(a), axis=0)


def product(both, weight, contract):
    rows = both.shape[0] // 2
    total = contract(both, weight)
    return total[:rows] + total[rows:]


def main_kernel(fields, z_ref, a_ref, b_ref, mix_ref, in_ref, b_in, down, side, out_h, out_l, out_hbm, *scratch):
    sum_s, corr_s, both_s, out_v, sems = scratch
    members, lons, half, embed = out_v.shape
    depth, count = out_h.shape
    rows = corr_s.shape[0]
    pad = in_ref.shape[0] // 3
    sum_s[...] = z_ref[...] + a_ref[...] + b_ref[...]
    cut = LANES // 2
    unpack(corr_s, sum_s, lons * half, (lons, half, cut, fields - cut))
    high, low = halves(corr_s[:, 0:fields])
    both_s[...] = jnp.zeros(both_s.shape, BF16)
    for k, part in enumerate((high, low, high)):
        both_s[:, k * pad : k * pad + fields] = part
    corr = both_s[:, 0 : 3 * pad]
    pre = dot(corr, in_ref[...]) + b_in[...]
    hidden = 0.5 * pre * (1.0 + lax.erf(pre * 0.7071067811865476))
    both = stacked(hidden[:, 0:depth])
    res = dot(corr, mix_ref[...])
    for k in range(down.shape[0]):
        res = res + hidden[:, depth + k : depth + k + 1] * down[k : k + 1, :]
    last = jnp.sum(hidden[:, 0:depth] * side[:, 0:depth], axis=1, keepdims=True)
    last = res[:, count : count + 1] + last
    stores = []
    for k, at in enumerate(range(0, count, 2 * LANES)):
        end = min(at + 2 * LANES, count)
        part = res[:, at:end] + product(both, out_h[:, at:end], dot) + dot(both[:rows], out_l[:, at:end])
        stop = embed if end == count else end
        for m in range(members):
            for n in range(lons):
                row = m * (rows // members) + n * half
                out_v[m, n, :, at:end] = part[row : row + half]
                if end == count:
                    out_v[m, n, :, end:stop] = last[row : row + half]
        view = pl.ds(at, stop - at)
        store = pltpu.make_async_copy(out_v.at[:, :, :, view], out_hbm.at[:, :, :, view], sems.at[k])
        store.start()
        stores.append(store)
    for store in stores:
        store.wait()


def per_device(state, kernels, kernel_index, w_mix, w_in, b_in, w_out):
    members, lat, fields, lons = state.shape
    half = lat // 2
    tiles = lons + members
    taps = kernels.shape[2]
    embed, ffn = w_in.shape
    step = SPACING // lons
    S, V = jax.ShapeDtypeStruct, pltpu.VMEM

    x = call(
        pack_kernel,
        out_shape=V((tiles, lat, LANES), F32),
        in_specs=[VMEM],
        out_specs=VMEM,
        name="pack",
    )(far(jnp.transpose(state, (0, 3, 1, 2))))
    left = ring(x, step)
    right = ring(x, -step)

    nearby, upper = call(
        taps_kernel,
        out_shape=[V((taps, 2, lat, LANES), F32)] * 2,
        in_specs=[SMEM, VMEM],
        out_specs=[VMEM] * 2,
        scratch_shapes=[V((taps, lat, fields), F32)] * 2,
        name="taps",
    )(far(kernel_index), far(jnp.transpose(kernels, (0, 2, 1, 3))))
    deep = -(-fields // 16) * 16
    mix_s, in_s = call(
        in_kernel,
        out_shape=[V((3 * deep, embed), BF16), V((3 * deep, ffn), BF16)],
        in_specs=[VMEM, ANY],
        out_specs=[VMEM] * 2,
        scratch_shapes=[V((2 * deep, embed), BF16), V((embed, ffn), F32), pltpu.SemaphoreType.DMA((-(-embed // 256),))],
        name="w_in",
    )(far(w_mix), far(w_in))
    bias = b_in.reshape(1, ffn)

    rows = tiles * half
    low, mid, high, halo = call(
        partial_kernel,
        out_shape=[V((rows, LANES), F32)] * 3 + [V((3 * tiles, LANES), F32)],
        in_specs=[VMEM] * 5 + [ANY],
        out_specs=[VMEM] * 4,
        scratch_shapes=[V((tiles * lat, LANES), F32), V(((tiles + 1) * lat, LANES), F32)],
        name="partial",
    )(near(x), near(left), near(right), near(nearby), near(upper), near(mix_s))
    above = next_band(halo)

    count, depth = embed // LANES * LANES, ffn // LANES * LANES
    out_h, out_l, down, side = call(
        out_kernel,
        out_shape=[V((depth, count), BF16)] * 2 + [V((ffn - depth, embed), F32), V((embed - count, ffn), F32)],
        in_specs=[VMEM, ANY],
        out_specs=[VMEM] * 4,
        name="w_out",
    )(near(jnp.transpose(w_out)), near(halo))
    low, mid, high = call(
        join_kernel,
        out_shape=[V((rows, LANES), F32)] * 3,
        in_specs=[VMEM] * 4 + [ANY],
        out_specs=[VMEM] * 3,
        input_output_aliases={0: 0, 1: 1, 2: 2},
        name="join",
    )(near(low), near(mid), near(high), near(above), near(side))
    from_low = ring(low, 3 * step)
    from_high = ring(high, -3 * step)

    pad = members * (-(-lons * half // 16) * 16)
    out = call(
        functools.partial(main_kernel, fields),
        out_shape=S((members, lons, half, embed), F32),
        in_specs=[VMEM] * 10,
        out_specs=ANY,
        scratch_shapes=[
            V((rows, LANES), F32),
            V((pad, LANES), F32),
            V((pad, 2 * LANES), BF16),
            V((members, lons, half, embed), F32),
            pltpu.SemaphoreType.DMA((-(-count // (2 * LANES)),)),
        ],
        name="main",
    )(*(near(a) for a in (mid, from_low, from_high, mix_s, in_s, bias, down, side, out_h, out_l)))
    return jnp.transpose(out, (0, 2, 1, 3))


def solution(mesh):
    placed = (P(None, "polar", None, "azimuth"), P(), P(), P(), P(), P(), P())
    return jax.shard_map(
        per_device,
        mesh=mesh,
        in_specs=placed,
        out_specs=P(None, "polar", "azimuth", None),
        check_vma=False,
    )
```
